256 devices in a mesh: cube: 4 (over y), grid: 64 (over z, x, core).
Axes of the slice: x: 4, y: 4, z: 8, core: 2. Of those that a mesh axis runs over, the one named last changes fastest.
Arguments:
- root_inverse: float32 [4096, 4096], P('grid', 'cube'), may hold values from -0.09375 to 0.09375
- level_inverse: float32 [1024, 2048], P('grid', 'cube'), may hold values from -0.1875 to 0.1875
- coupling: float32 [4096, 2048], P('grid', 'cube'), may hold values from -0.1875 to 0.1875
- pattern: int32 [2, 32], replicated, may hold values 0 or 1
Outputs:
- root_cov: float32 [4096, 4096], P('grid', 'cube')
- cross_cov: float32 [4096, 2048], P('grid', 'cube')
- node_cov: float32 [1024, 2048], P('grid', 'cube')
The draws below stay inside these ranges and needn't reach their ends.
All inputs are finite; a program needn't handle non-finite values.
Results may differ from the reference program's by a relative error of at most 0.0001.
Values sent between devices are 32-bit elements; how exact they have to be, the bound alone decides.
No kernel may reach another device: no remote copies, remote signals or barrier semaphores. Data moves between devices by JAX's collectives and lax.ppermute only.
A program may use at most 128 MiB of HBM per device.

```python
import jax
import jax.numpy as jnp
from jax import lax

NR = 4096
N1 = 1024
BLK = 128


def plant(array, key, low, top_value):
    longest = array.shape.index(max(array.shape))
    spots = []
    for shift in (0, 1):
        where = [jax.random.randint(jax.random.fold_in(key, axis), (), 0, length) for axis, length in enumerate(array.shape)]
        where[longest] = (where[longest] + shift) % array.shape[longest]
        spots.append(tuple(where))
    return array.at[spots[0]].set(low).at[spots[1]].set(top_value)


def shard_levels(key, extent, split, least, largest):
    level, own = 1.0, jax.random.fold_in(key, 6)
    for axis_at, blocks in split:
        draws = jnp.exp(jax.random.uniform(jax.random.fold_in(own, axis_at), (blocks,), jnp.float32, least / len(split), largest / len(split)))
        level = level * jnp.repeat(draws, extent[axis_at] // blocks).reshape([-1 if axis == axis_at else 1 for axis in range(len(extent))])
    return level


def noise(own_key, extent, spread, most, split=(), kind=jnp.bfloat16):
    drawn = spread * jax.random.normal(own_key, extent, jnp.float32)
    if split:
        drawn = drawn * shard_levels(own_key, extent, split, -0.22, 0.18)
    return jnp.clip(drawn, -most, most).astype(kind)


def setup_inputs(seed: int = 0) -> dict:
    key_of = jax.random.split(jax.random.key(seed), 5)
    root_inverse = noise(key_of[0], (NR, NR), NR ** -0.5, 0.09375, ((0, 64), (1, 4)), jnp.float32)
    level_inverse = noise(key_of[1], (N1, 2 * N1), N1 ** -0.5, 0.1875, ((0, 64), (1, 4)), jnp.float32)
    coupling = noise(key_of[2], (NR, 2 * N1), (NR // 4) ** -0.5, 0.1875, ((0, 64), (1, 4)), jnp.float32)
    pattern = plant((jax.random.randint(key_of[3], (2, NR // BLK), 0, 2) < 1).astype(jnp.int32), jax.random.fold_in(key_of[3], 1), 0, 1)
    return {"root_inverse": root_inverse, "level_inverse": level_inverse, "coupling": coupling, "pattern": pattern}


HIGHEST = lax.Precision.HIGHEST


def product(left, right):
    return jnp.dot(left, right, precision=HIGHEST, preferred_element_type=jnp.float32)


def lower_unit(weights, order):
    return jnp.tril(weights, -1) + jnp.eye(order, dtype=weights.dtype)


def reference(root_inverse, level_inverse, coupling, pattern):
    root_lower = lower_unit(root_inverse, NR)
    root_cov = product(root_lower.T, root_lower)
    masks = jnp.repeat(pattern.astype(jnp.float32), BLK, axis=1)
    cross_list = []
    node_list = []
    for node in range(2):
        node_lower = lower_unit(level_inverse[:, node * N1:(node + 1) * N1], N1)
        row_mask = masks[node][:, None]
        coupled = coupling[:, node * N1:(node + 1) * N1] * row_mask
        factor = product(coupled, node_lower)
        cross = -product(root_cov, factor) * row_mask
        node_cov = product(node_lower.T, node_lower) - product(factor.T, cross)
        cross_list.append(cross)
        node_list.append(node_cov)
    return root_cov, jnp.concatenate(cross_list, axis=1), jnp.concatenate(node_list, axis=1)
```

```python
import jax
import jax.numpy as jnp
from jax import lax
from jax.sharding import Mesh, PartitionSpec as P

BLK = 128
HIGHEST = lax.Precision.HIGHEST
XC = ("x", "c")


def shifted(value, axis, step):
    size = lax.axis_size(axis)
    return lax.ppermute(value, axis, [(i, (i + step) % size) for i in range(size)])


def from_partner(value, axis):
    return lax.ppermute(value, axis, [(i, i ^ 1) for i in range(lax.axis_size(axis))])


def gather(value, axis):
    size, me = lax.axis_size(axis), lax.axis_index(axis)
    out = jnp.zeros((size, *value.shape), value.dtype)
    rest = (0,) * value.ndim
    moved = [value] + [shifted(value, axis, step) for step in range(1, size)]
    for step, block in enumerate(moved):
        out = lax.dynamic_update_slice(out, block[None], ((me - step) % size, *rest))
    return out


def contract(spec, left, right):
    return jnp.einsum(spec, left, right, precision=HIGHEST, preferred_element_type=jnp.float32)


def lower_piece(weights, row_start, col_start):
    rows = row_start + lax.broadcasted_iota(jnp.int32, weights.shape, 0)
    cols = col_start + lax.broadcasted_iota(jnp.int32, weights.shape, 1)
    below = jnp.where(cols < rows, weights, jnp.zeros_like(weights))
    return below + jnp.where(cols == rows, 1.0, 0.0).astype(jnp.float32)


def join_halves(own, other, half, axis):
    first = jnp.concatenate([own, other], axis=axis)
    second = jnp.concatenate([other, own], axis=axis)
    return jnp.where(half == 0, first, second)


def on_device(root_inverse, level_inverse, coupling, pattern):
    y, z, x, c = (lax.axis_index(name) for name in ("y", "z", "x", "c"))
    ny, nz, nxc = lax.axis_size("y"), lax.axis_size("z"), lax.axis_size("x") * lax.axis_size("c")
    xc = x * lax.axis_size("c") + c
    grid_index = z * nxc + xc
    node, half = y // 2, y % 2
    rows, cols = root_inverse.shape
    node_rows, width = level_inverse.shape
    per_y = cols // (rows * nxc)

    root_lower = lower_piece(root_inverse, grid_index * rows, y * cols)
    node_lower = lower_piece(level_inverse, grid_index * node_rows, half * width)
    row_mask = pattern[node, grid_index * rows // BLK].astype(jnp.float32)

    coupled = gather(coupling * row_mask, "z").reshape(ny, per_y * rows, width)
    pieces = root_lower.reshape(rows, per_y, nxc, rows).transpose(2, 0, 1, 3).reshape(1, nxc, rows, per_y * rows)
    pieces = jnp.broadcast_to(pieces, (ny, *pieces.shape[1:])).reshape(ny * nxc, rows, per_y * rows)
    lower = lax.all_to_all(pieces, ("y", *XC), 0, 0, tiled=True).reshape(ny, nxc * rows, per_y * rows)
    lower_rows = lax.all_gather(root_lower, XC, axis=0, tiled=True)
    node_all = lax.all_gather(gather(node_lower, "z"), XC, axis=1, tiled=True)
    node_all = node_all.reshape(nz * nxc * node_rows, width)

    partial = contract("yrm,ymj->rj", lower, coupled).reshape(nxc, rows, width)
    mixed = jnp.sum(lax.all_to_all(partial, XC, 0, 0, tiled=True), axis=0)
    mixed = join_halves(mixed, from_partner(mixed, "y"), half, 1)
    solved = contract("rm,mj->rj", mixed, node_all)
    swapped = gather(solved, "x").reshape(-1, 1, rows, width)
    other = from_partner(swapped, "c")
    solved = join_halves(swapped, other, c, 1).reshape(nxc * rows, width)

    root = contract("yrm,rj->ymj", lower, lower_rows).reshape(nz * rows, cols)
    root_cov = lax.psum_scatter(root, "z", scatter_dimension=0, tiled=True)

    cross = contract("yrm,rj->ymj", lower, solved).reshape(nz, rows, width)
    own = lax.dynamic_index_in_dim(
        solved.reshape(nxc * rows, nz // 2, nxc, node_rows), xc, 2, keepdims=False
    ).reshape(nxc * rows, nz // 2 * node_rows)
    chosen = join_halves(own, from_partner(own, "y"), half, 1)
    gram = contract("rm,rj->mj", chosen, solved).reshape(nz, node_rows, width)
    both = jnp.concatenate([cross, gram], axis=1)
    both = lax.psum_scatter(both, "z", scatter_dimension=0, tiled=True)[0]
    cross_cov = -(both[:rows] * row_mask)
    mine = lax.dynamic_slice_in_dim(node_all, grid_index % (width // node_rows) * node_rows, node_rows, 1).T
    mine = jnp.where(grid_index // (width // node_rows) == half, mine, from_partner(mine, "y"))
    node_cov = contract("im,mj->ij", mine, node_all) + both[rows:]
    return root_cov, cross_cov, node_cov


def solution(mesh):
    split = Mesh(mesh.devices.reshape(4, 8, 4, 2), ("y", "z", "x", "c"))
    placed = P(("z", "x", "c"), "y")
    return jax.shard_map(
        on_device,
        mesh=split,
        in_specs=(placed, placed, placed, P()),
        out_specs=(placed, placed, placed),
        check_vma=False,
    )
```

```python
import jax
import jax.numpy as jnp
from jax import lax
from jax.experimental import pallas as pl
from jax.experimental.pallas import tpu as pltpu
from jax.sharding import Mesh, PartitionSpec as P

BLK = 128
NY, NZ, NX, NC = 4, 8, 4, 2
NXC = NX * NC
F32 = jnp.float32


def shifted(value, axis, step):
    size = lax.axis_size(axis)
    return lax.ppermute(value, axis, [(i, (i + step) % size) for i in range(size)])


def from_partner(value, axis):
    return lax.ppermute(value, axis, [(i, i ^ 1) for i in range(lax.axis_size(axis))])


def chip_blocks(value):
    own = [value] + [shifted(value, "x", s) for s in range(1, NX)]
    return own + [from_partner(block, "c") for block in own]


def halves(value):
    high = value.astype(jnp.bfloat16)
    return high, (value - high.astype(F32)).astype(jnp.bfloat16)


def product(left, right, contracting):
    (high, low), (right_high, right_low) = halves(left), halves(right)

    def dot(p, q):
        return lax.dot_general(p, q, (contracting, ((), ())), preferred_element_type=F32)

    return dot(high, right_high) + (dot(high, right_low) + dot(low, right_high))


ROWS = ((1,), (0,))
COLS = ((0,), (0,))


def call(body, outs, scratch=(), n_in=1, aliases=None, in_specs=None, out_specs=None, grid=(), copies=0):
    vmem = pl.BlockSpec(memory_space=pltpu.VMEM)
    smem = pl.BlockSpec(memory_space=pltpu.SMEM)
    return pl.pallas_call(
        body,
        out_shape=[jax.ShapeDtypeStruct(shape, F32) for shape in outs],
        in_specs=in_specs or [smem] + [vmem] * n_in,
        out_specs=out_specs or [vmem] * len(outs),
        grid=grid,
        scratch_shapes=[pltpu.VMEM(shape, F32) for shape in scratch]
        + ([pltpu.SemaphoreType.DMA((copies,))] if copies else []),
        input_output_aliases=aliases or {},
        compiler_params=pltpu.CompilerParams(vmem_limit_bytes=48 * 2**20),
    )


def lower_piece(weights, row_start, col_start):
    rows = row_start + lax.broadcasted_iota(jnp.int32, weights.shape, 0)
    cols = col_start + lax.broadcasted_iota(jnp.int32, weights.shape, 1)
    below = jnp.where(cols < rows, weights, 0.0)
    return below + jnp.where(cols == rows, 1.0, 0.0).astype(F32)


def row_mask(at, pattern, rows):
    block = (at[1] * NXC + at[2] * NC + at[3]) * rows // BLK
    return pattern[at[0] // 2, block].astype(F32)


def stack_rows(at, pattern, level, coupling, after, stacks, nodes, rows_in, sem):
    del after
    moves = [pltpu.make_async_copy(level, nodes, sem.at[0]), pltpu.make_async_copy(coupling, rows_in, sem.at[1])]
    for move in moves:
        move.start()
    for move in moves:
        move.wait()
    rows, g = coupling.shape[0], at[1] * NXC + at[2] * NC + at[3]
    masked = rows_in[...] * row_mask(at, pattern, rows)
    low = lower_piece(nodes[...], g * level.shape[0], at[0] % 2 * level.shape[1])
    for to in range(NZ):
        stacks[to, :rows] = masked
        stacks[to, rows:] = low


def root_columns(at, *refs):
    blocks, (whole, columns) = refs[:NXC], refs[NXC:]
    rows, cols = blocks[0].shape
    for k, block in enumerate(blocks):
        core = at[3] if k < NX else 1 - at[3]
        place = lax.rem(at[2] + NX - k % NX, NX) * NC + core
        low = lower_piece(block[...], (at[1] * NXC + place) * rows, at[0] * cols)
        whole[pl.ds(pl.multiple_of(place * rows, rows), rows)] = low
    parts = []
    for b in range(0, cols, NXC * rows):
        pair = whole[:, pl.ds(pl.multiple_of(b + at[2] * NC * rows, NC * rows), NC * rows)]
        parts.append(jnp.where(at[3] == 0, pair[:, :rows], pair[:, rows:]))
    columns[...] = jnp.concatenate(parts, axis=1)


def whole_lower(columns):
    return jnp.concatenate([block[...] for block in columns], axis=1)


def place_chip_blocks(at, blocks, out):
    rows = blocks[0].shape[0]
    for k, block in enumerate(blocks):
        s, core = k % NX, at[3] if k < NX else 1 - at[3]
        chip = lax.rem(at[2] + NX - s, NX)
        out[pl.ds(pl.multiple_of((chip * NC + core) * rows, rows), rows)] = block[...]


def mix(at, *refs):
    columns, stacks, (keep, give, nodes, full, part) = refs[:NY], refs[NY], refs[NY + 2:]
    rows, per_y = keep.shape[1], NZ // NY
    for s in range(NY):
        k = lax.rem(at[0] + NY - s, NY) * per_y
        for b in range(per_y):
            full[(s * per_y + b) * rows:(s * per_y + b + 1) * rows] = stacks[k + b, :rows]
    nodes[...] = stacks[:, rows:]
    part[...] = product(whole_lower(columns), full[...], ROWS)
    for s in range(NX):
        chip = lax.rem(at[2] + NX - s, NX)
        for core, out in ((at[3], keep), (1 - at[3], give)):
            out[s] = part[pl.ds(pl.multiple_of((chip * NC + core) * rows, rows), rows)]


def add_cores(at, keep, got, *outs):
    for s, out in enumerate(outs):
        out[...] = keep[s] + got[s]


def whole_node(at, *refs):
    blocks, out = refs[:NXC], refs[NXC]
    for k, block in enumerate(blocks):
        s, core = k % NX, at[3] if k < NX else 1 - at[3]
        chip = lax.rem(at[2] + NX - s, NX)
        for b in range(NZ):
            out[b, chip * NC + core] = block[b]


def solve(at, own, other, node, out):
    half = at[0] % 2
    width = own.shape[1]
    first = node[pl.ds(pl.multiple_of(half * width, width), width)]
    second = node[pl.ds(pl.multiple_of((1 - half) * width, width), width)]
    out[...] = product(own[...], first, ROWS) + product(other[...], second, ROWS)


def store_by_y(at, value, out, rows):
    per_y = NZ // NY
    for s in range(NY):
        k = lax.rem(at[0] + NY - s, NY) * per_y
        for b in range(per_y):
            at_row = (s * per_y + b) * rows
            out[k + b, :rows] = value[at_row:at_row + rows]


def root_product(at, *refs):
    columns, (whole, out) = refs[:NY], refs[NY:]
    store_by_y(at, product(whole_lower(columns), whole[...], COLS), out, out.shape[1])


def choose(at, *refs):
    blocks, (out, full) = refs[:NXC], refs[NXC:]
    place_chip_blocks(at, blocks, full)
    size, take = out.shape[0], out.shape[1] // 2
    node_rows = take * 2 // NZ
    src = lax.broadcasted_iota(jnp.int32, (full.shape[1], take), 0)
    dst = lax.broadcasted_iota(jnp.int32, (full.shape[1], take), 1)
    pick = src == dst // node_rows * (NXC * node_rows) + (at[2] * NC + at[3]) * node_rows + dst % node_rows
    taken = product(full[...], jnp.where(pick, 1.0, 0.0).astype(F32), ROWS)
    out[...] = jnp.concatenate([taken[:size], taken[size:]], axis=1)


def cross_product(at, *refs):
    columns, blocks, (out, full) = refs[:NY], refs[NY:NY + NXC], refs[NY + NXC:]
    place_chip_blocks(at, blocks, full)
    store_by_y(at, product(whole_lower(columns), full[...], COLS), out, blocks[0].shape[0])


def gram_product(at, own, other, *refs):
    blocks, (_, out, full) = refs[:NXC], refs[NXC:]
    place_chip_blocks(at, blocks, full)
    first, take = (at[0] % 2) == 0, own.shape[1] // 2
    mine, his = own[...], other[...]
    low, high = jnp.where(first, mine, his), jnp.where(first, his, mine)
    chosen = jnp.concatenate(
        [
            jnp.concatenate([low[:, :take], high[:, :take]], axis=1),
            jnp.concatenate([low[:, take:], high[:, take:]], axis=1),
        ],
        axis=0,
    )
    out[...] = product(chosen, full[...], COLS).reshape(out.shape)


def finish(at, pattern, got, gram, cross, node):
    total = got[0]
    for k in range(1, NZ):
        total = total + got[k]
    rows = cross.shape[0]
    cross[...] = -(total[:rows] * row_mask(at, pattern, rows))
    node[...] = gram[...] + total[rows:]


def on_device(root_inverse, level_inverse, coupling, pattern):
    y, z, x, c = (lax.axis_index(name) for name in ("y", "z", "x", "c"))
    grid_index = z * NXC + x * NC + c
    half = y % 2
    rows, cols = root_inverse.shape
    node_rows, width = level_inverse.shape
    at = jnp.stack([y, z, x, c]).astype(jnp.int32)
    per = rows + node_rows
    smem, vmem, anywhere = (pl.BlockSpec(memory_space=m) for m in (pltpu.SMEM, pltpu.VMEM, pl.ANY))

    blocks = chip_blocks(root_inverse)
    stacks = call(
        stack_rows,
        [(NZ, per, width)],
        [(node_rows, width), (rows, width)],
        in_specs=[smem, smem, anywhere, anywhere, anywhere],
        copies=2,
    )(at, pattern, level_inverse, coupling, level_inverse)[0]
    stacks = lax.all_to_all(stacks, "z", 0, 0, tiled=True)
    whole, columns = call(root_columns, [(NXC * rows, cols), (NXC * rows, cols // NXC)], n_in=NXC)(
        at, *blocks
    )
    columns = [columns] + [shifted(columns, "y", s) for s in range(1, NY)]

    root = call(root_product, [(NZ, rows, cols)], n_in=NY + 1)(
        at, *columns, whole
    )[0]
    summed = lax.all_to_all(root, "z", 0, 0, tiled=True)

    keep, give, nodes = call(
        mix,
        [(NX, rows, width), (NX, rows, width), (NZ, node_rows, width)],
        [(NZ * rows, width), (NXC * rows, width)],
        in_specs=[smem] + [vmem] * (NY + 1) + [anywhere],
    )(at, *columns, stacks, root)
    parts = call(add_cores, [(rows, width)] * NX, n_in=2)(at, keep, from_partner(give, "c"))
    mixed = parts[0]
    for s in range(1, NX):
        mixed = mixed + shifted(parts[s], "x", -s)

    node_all = call(whole_node, [(NZ, NXC, node_rows, width)], n_in=NXC)(at, *chip_blocks(nodes))[0]
    node_all = node_all.reshape(NZ * NXC * node_rows, width)
    solved = call(solve, [(rows, width)], n_in=3)(at, mixed, from_partner(mixed, "y"), node_all)[0]
    solved = chip_blocks(solved)

    own = call(choose, [(NX * rows, 2 * width // NXC)], [(NXC * rows, width)], NXC)(at, *solved)[0]
    both = call(cross_product, [(NZ, per, width)], [(NXC * rows, width)], NY + NXC)(at, *columns, *solved)[0]
    both = call(
        gram_product,
        [(NZ, per, width)],
        [(NXC * rows, width)],
        aliases={3 + NXC: 0},
        in_specs=[smem] + [vmem] * (2 + NXC) + [anywhere],
        out_specs=[pl.BlockSpec((NZ, node_rows, width), lambda i: (0, rows // node_rows, 0))],
        grid=(1,),
    )(at, own, from_partner(own, "y"), *solved, both)[0]
    both, summed = lax.optimization_barrier((both, summed))
    both = lax.all_to_all(both, "z", 0, 0, tiled=True)

    per_half = width // node_rows
    mine = lax.dynamic_slice_in_dim(node_all, grid_index % per_half * node_rows, node_rows, 1).T
    mine = jnp.where(grid_index // per_half == half, mine, from_partner(mine, "y"))
    node_gram = jnp.dot(mine, node_all, precision=lax.Precision.HIGHEST, preferred_element_type=F32)
    cross_cov, node_cov = call(finish, [(rows, width), (node_rows, width)], in_specs=[smem, smem, vmem, vmem])(
        at, pattern, both, node_gram
    )
    return jnp.sum(summed, axis=0), cross_cov, node_cov


def solution(mesh):
    split = Mesh(mesh.devices.reshape(NY, NZ, NX, NC), ("y", "z", "x", "c"))
    placed = P(("z", "x", "c"), "y")
    return jax.shard_map(
        on_device,
        mesh=split,
        in_specs=(placed, placed, placed, P()),
        out_specs=(placed, placed, placed),
        check_vma=False,
    )
```

```python
import jax
import jax.numpy as jnp
from jax import lax
from jax.experimental import pallas as pl
from jax.experimental.pallas import tpu as pltpu
from jax.sharding import Mesh, PartitionSpec as P

BLK = 128
NY, NZ, NX, NC = 4, 8, 4, 2
NXC = NX * NC
F32 = jnp.float32


def shifted(value, axis, step):
    size = lax.axis_size(axis)
    return lax.ppermute(value, axis, [(i, (i + step) % size) for i in range(size)])


def from_partner(value, axis):
    return lax.ppermute(value, axis, [(i, i ^ 1) for i in range(lax.axis_size(axis))])


def chip_blocks(value):
    own = [value] + [shifted(value, "x", s) for s in range(1, NX)]
    return own + [from_partner(block, "c") for block in own]


def halves(value):
    high = value.astype(jnp.bfloat16)
    return high, (value - high.astype(F32)).astype(jnp.bfloat16)


def product(left, right, contracting):
    (high, low), (right_high, right_low) = halves(left), halves(right)

    def dot(p, q):
        return lax.dot_general(p, q, (contracting, ((), ())), preferred_element_type=F32)

    return dot(high, right_high) + (dot(high, right_low) + dot(low, right_high))


ROWS = ((1,), (0,))
COLS = ((0,), (0,))


def call(body, outs, scratch=(), n_in=1, aliases=None, in_specs=None, out_specs=None, grid=(), copies=0):
    vmem = pl.BlockSpec(memory_space=pltpu.VMEM)
    smem = pl.BlockSpec(memory_space=pltpu.SMEM)
    return pl.pallas_call(
        body,
        out_shape=[jax.ShapeDtypeStruct(shape, F32) for shape in outs],
        in_specs=in_specs or [smem] + [vmem] * n_in,
        out_specs=out_specs or [vmem] * len(outs),
        grid=grid,
        scratch_shapes=[pltpu.VMEM(shape, F32) for shape in scratch]
        + ([pltpu.SemaphoreType.DMA((copies,))] if copies else []),
        input_output_aliases=aliases or {},
        compiler_params=pltpu.CompilerParams(vmem_limit_bytes=48 * 2**20),
    )


def lower_piece(weights, row_start, col_start):
    rows = row_start + lax.broadcasted_iota(jnp.int32, weights.shape, 0)
    cols = col_start + lax.broadcasted_iota(jnp.int32, weights.shape, 1)
    below = jnp.where(cols < rows, weights, 0.0)
    return below + jnp.where(cols == rows, 1.0, 0.0).astype(F32)


def row_mask(at, z, pattern, rows):
    return pattern[at[0] // 2, (z * NXC + at[2] * NC + at[3]) * rows // BLK].astype(F32)


def root_columns(at, *refs):
    blocks, (whole, columns) = refs[:NXC], refs[NXC:]
    rows, cols = blocks[0].shape
    for k, block in enumerate(blocks):
        core = at[3] if k < NX else 1 - at[3]
        place = lax.rem(at[2] + NX - k % NX, NX) * NC + core
        low = lower_piece(block[...], (at[1] * NXC + place) * rows, at[0] * cols)
        whole[pl.ds(pl.multiple_of(place * rows, rows), rows)] = low
    parts = []
    for b in range(0, cols, NXC * rows):
        pair = whole[:, pl.ds(pl.multiple_of(b + at[2] * NC * rows, NC * rows), NC * rows)]
        parts.append(jnp.where(at[3] == 0, pair[:, :rows], pair[:, rows:]))
    columns[...] = jnp.concatenate(parts, axis=1)


def whole_lower(columns):
    return jnp.concatenate([block[...] for block in columns], axis=1)


def place_chip_blocks(at, blocks, out):
    rows = blocks[0].shape[0]
    for k, block in enumerate(blocks):
        s, core = k % NX, at[3] if k < NX else 1 - at[3]
        chip = lax.rem(at[2] + NX - s, NX)
        out[pl.ds(pl.multiple_of((chip * NC + core) * rows, rows), rows)] = block[...]


def take_nodes(at, stacks, nodes, sem):
    move = pltpu.make_async_copy(stacks.at[:, stacks.shape[1] - nodes.shape[1]:], nodes, sem.at[0])
    move.start()
    move.wait()


def mix(at, pattern, *refs):
    columns, stacks, (keep, give, full, part) = refs[:NY], refs[NY], refs[NY + 2:]
    rows, per_y = keep.shape[1], NZ // NY
    for s in range(NY):
        k = lax.rem(at[0] + NY - s, NY) * per_y
        for b in range(per_y):
            full[(s * per_y + b) * rows:(s * per_y + b + 1) * rows] = stacks[k + b, :rows] * row_mask(at, k + b, pattern, rows)
    part[...] = product(whole_lower(columns), full[...], ROWS)
    for s in range(NX):
        chip = lax.rem(at[2] + NX - s, NX)
        for core, out in ((at[3], keep), (1 - at[3], give)):
            out[s] = part[pl.ds(pl.multiple_of((chip * NC + core) * rows, rows), rows)]


def add_cores(at, keep, got, *outs):
    for s, out in enumerate(outs):
        out[...] = keep[s] + got[s]


def whole_node(at, *refs):
    blocks, out = refs[:NXC], refs[NXC]
    for k, block in enumerate(blocks):
        s, core = k % NX, at[3] if k < NX else 1 - at[3]
        chip = lax.rem(at[2] + NX - s, NX)
        count, width = block.shape[1:]
        for b in range(NZ):
            place = chip * NC + core
            out[b, place] = lower_piece(block[b], (b * NXC + place) * count, at[0] % 2 * width)


def solve(at, own, other, node, out):
    half = at[0] % 2
    width = own.shape[1]
    first = node[pl.ds(pl.multiple_of(half * width, width), width)]
    second = node[pl.ds(pl.multiple_of((1 - half) * width, width), width)]
    out[...] = product(own[...], first, ROWS) + product(other[...], second, ROWS)


def store_by_y(at, value, out, rows):
    per_y = NZ // NY
    for s in range(NY):
        k = lax.rem(at[0] + NY - s, NY) * per_y
        for b in range(per_y):
            at_row = (s * per_y + b) * rows
            out[k + b, :rows] = value[at_row:at_row + rows]


def root_part(at, first, columns, whole, out, part, sem):
    rows, per_y = out.shape[1], NZ // NY
    part[...] = product(whole_lower(columns), whole[...], COLS)
    moves = []
    for s in range(len(columns)):
        k = lax.rem(at[0] + NY - s - first, NY) * per_y
        for b in range(per_y):
            from_rows = part.at[pl.ds((s * per_y + b) * rows, rows)]
            moves.append(pltpu.make_async_copy(from_rows, out.at[k + b], sem.at[len(moves)]))
            moves[-1].start()
    for move in moves:
        move.wait()


def root_product(at, *refs):
    root_part(at, 0, refs[:NY // 2], *refs[NY // 2:])


def root_rest(at, *refs):
    columns, whole, _, out, part, sem = refs[:NY // 2], *refs[NY // 2:]
    root_part(at, NY // 2, columns, whole, out, part, sem)


def choose(at, *refs):
    blocks, (out, full) = refs[:NXC], refs[NXC:]
    place_chip_blocks(at, blocks, full)
    size, take = out.shape[0], out.shape[1] // 2
    node_rows = take * 2 // NZ
    src = lax.broadcasted_iota(jnp.int32, (full.shape[1], take), 0)
    dst = lax.broadcasted_iota(jnp.int32, (full.shape[1], take), 1)
    pick = src == dst // node_rows * (NXC * node_rows) + (at[2] * NC + at[3]) * node_rows + dst % node_rows
    taken = product(full[...], jnp.where(pick, 1.0, 0.0).astype(F32), ROWS)
    out[...] = jnp.concatenate([taken[:size], taken[size:]], axis=1)


def cross_product(at, *refs):
    columns, blocks, (out, full) = refs[:NY], refs[NY:NY + NXC], refs[NY + NXC:]
    place_chip_blocks(at, blocks, full)
    store_by_y(at, product(whole_lower(columns), full[...], COLS), out, blocks[0].shape[0])


def gram_product(at, own, other, *refs):
    blocks, (_, out, full) = refs[:NXC], refs[NXC:]
    place_chip_blocks(at, blocks, full)
    first, take = (at[0] % 2) == 0, own.shape[1] // 2
    mine, his = own[...], other[...]
    low, high = jnp.where(first, mine, his), jnp.where(first, his, mine)
    chosen = jnp.concatenate(
        [
            jnp.concatenate([low[:, :take], high[:, :take]], axis=1),
            jnp.concatenate([low[:, take:], high[:, take:]], axis=1),
        ],
        axis=0,
    )
    out[...] = product(chosen, full[...], COLS).reshape(out.shape)


def finish(at, pattern, got, gram, cross, node):
    total = got[0]
    for k in range(1, NZ):
        total = total + got[k]
    rows = cross.shape[0]
    cross[...] = -(total[:rows] * row_mask(at, at[1], pattern, rows))
    node[...] = gram[...] + total[rows:]


def on_device(root_inverse, level_inverse, coupling, pattern):
    y, z, x, c = (lax.axis_index(name) for name in ("y", "z", "x", "c"))
    grid_index = z * NXC + x * NC + c
    half = y % 2
    rows, cols = root_inverse.shape
    node_rows, width = level_inverse.shape
    at = jnp.stack([y, z, x, c]).astype(jnp.int32)
    per = rows + node_rows
    smem, vmem, anywhere = (pl.BlockSpec(memory_space=m) for m in (pltpu.SMEM, pltpu.VMEM, pl.ANY))
    outside = pl.BlockSpec(memory_space=pltpu.HBM)

    blocks = chip_blocks(root_inverse)
    stacks = jnp.broadcast_to(jnp.concatenate([coupling, level_inverse])[None], (NZ, per, width))
    stacks = lax.all_to_all(stacks, "z", 0, 0, tiled=True)
    nodes = call(take_nodes, [(NZ, node_rows, width)], in_specs=[smem, anywhere], copies=1)(at, stacks)[0]
    nodes = chip_blocks(nodes)
    whole, columns = call(root_columns, [(NXC * rows, cols), (NXC * rows, cols // NXC)], n_in=NXC)(
        at, *blocks
    )
    columns = [columns] + [shifted(columns, "y", s) for s in range(1, NY)]

    shape, part = [(NZ, rows, cols)], [(NZ // 2 * rows, cols)]
    root = call(
        root_product, shape, part, NY // 2 + 1, out_specs=[outside], copies=NZ // 2
    )(at, *columns[:NY // 2], whole)[0]
    root = call(
        root_rest,
        shape,
        part,
        in_specs=[smem] + [vmem] * (NY // 2 + 1) + [outside],
        out_specs=[outside],
        aliases={NY // 2 + 2: 0},
        copies=NZ // 2,
    )(at, *columns[NY // 2:], whole, root)[0]
    summed = lax.all_to_all(root, "z", 0, 0, tiled=True)

    keep, give = call(
        mix,
        [(NX, rows, width)] * 2,
        [(NZ * rows, width), (NXC * rows, width)],
        in_specs=[smem, smem] + [vmem] * (NY + 1) + [anywhere],
    )(at, pattern, *columns, stacks, root)
    parts = call(add_cores, [(rows, width)] * NX, n_in=2)(at, keep, from_partner(give, "c"))
    mixed = parts[0]
    for s in range(1, NX):
        mixed = mixed + shifted(parts[s], "x", -s)

    node_all = call(whole_node, [(NZ, NXC, node_rows, width)], n_in=NXC)(at, *nodes)[0]
    node_all = node_all.reshape(NZ * NXC * node_rows, width)
    solved = call(solve, [(rows, width)], n_in=3)(at, mixed, from_partner(mixed, "y"), node_all)[0]
    solved = chip_blocks(solved)

    own = call(choose, [(NX * rows, 2 * width // NXC)], [(NXC * rows, width)], NXC)(at, *solved)[0]
    both = call(cross_product, [(NZ, per, width)], [(NXC * rows, width)], NY + NXC)(at, *columns, *solved)[0]
    both = call(
        gram_product,
        [(NZ, per, width)],
        [(NXC * rows, width)],
        aliases={3 + NXC: 0},
        in_specs=[smem] + [vmem] * (2 + NXC) + [anywhere],
        out_specs=[pl.BlockSpec((NZ, node_rows, width), lambda i: (0, rows // node_rows, 0))],
        grid=(1,),
    )(at, own, from_partner(own, "y"), *solved, both)[0]
    both, summed = lax.optimization_barrier((both, summed))
    both = lax.all_to_all(both, "z", 0, 0, tiled=True)

    per_half = width // node_rows
    mine = lax.dynamic_slice_in_dim(node_all, grid_index % per_half * node_rows, node_rows, 1).T
    mine = jnp.where(grid_index // per_half == half, mine, from_partner(mine, "y"))
    node_gram = jnp.dot(mine, node_all, precision=lax.Precision.HIGHEST, preferred_element_type=F32)
    cross_cov, node_cov = call(finish, [(rows, width), (node_rows, width)], in_specs=[smem, smem, vmem, vmem])(
        at, pattern, both, node_gram
    )
    return jnp.sum(summed, axis=0), cross_cov, node_cov


def solution(mesh):
    split = Mesh(mesh.devices.reshape(NY, NZ, NX, NC), ("y", "z", "x", "c"))
    placed = P(("z", "x", "c"), "y")
    return jax.shard_map(
        on_device,
        mesh=split,
        in_specs=(placed, placed, placed, P()),
        out_specs=(placed, placed, placed),
        check_vma=False,
    )
```

```python
import jax
import jax.numpy as jnp
from jax import lax
from jax.experimental import pallas as pl
from jax.experimental.pallas import tpu as pltpu
from jax.sharding import Mesh, PartitionSpec as P

BLK = 128
NY, NZ, NX, NC = 4, 8, 4, 2
NXC = NX * NC
F32 = jnp.float32


def shifted(value, axis, step):
    size = lax.axis_size(axis)
    return lax.ppermute(value, axis, [(i, (i + step) % size) for i in range(size)])


def from_partner(value, axis):
    return lax.ppermute(value, axis, [(i, i ^ 1) for i in range(lax.axis_size(axis))])


def chip_blocks(value):
    own = [value] + [shifted(value, "x", s) for s in range(1, NX)]
    return own + [from_partner(block, "c") for block in own]


def halves(value):
    high = value.astype(jnp.bfloat16)
    return high, (value - high.astype(F32)).astype(jnp.bfloat16)


def product(left, right, contracting):
    (high, low), (right_high, right_low) = halves(left), halves(right)

    def dot(p, q):
        return lax.dot_general(p, q, (contracting, ((), ())), preferred_element_type=F32)

    return dot(high, right_high) + (dot(high, right_low) + dot(low, right_high))


ROWS = ((1,), (0,))
COLS = ((0,), (0,))


def call(body, outs, scratch=(), n_in=1, aliases=None, in_specs=None, out_specs=None, grid=(), copies=0, weight=0):
    vmem = pl.BlockSpec(memory_space=pltpu.VMEM)
    smem = pl.BlockSpec(memory_space=pltpu.SMEM)
    return pl.pallas_call(
        body,
        out_shape=[jax.ShapeDtypeStruct(shape, F32) for shape in outs],
        in_specs=in_specs or [smem] + [vmem] * n_in,
        out_specs=out_specs or [vmem] * len(outs),
        grid=grid,
        scratch_shapes=[pltpu.VMEM(shape, F32) for shape in scratch]
        + ([pltpu.SemaphoreType.DMA((copies,))] if copies else []),
        input_output_aliases=aliases or {},
        cost_estimate=pl.CostEstimate(flops=weight, transcendentals=0, bytes_accessed=0) if weight else None,
        compiler_params=pltpu.CompilerParams(vmem_limit_bytes=48 * 2**20),
    )


def lower_piece(weights, row_start, col_start):
    rows = row_start + lax.broadcasted_iota(jnp.int32, weights.shape, 0)
    cols = col_start + lax.broadcasted_iota(jnp.int32, weights.shape, 1)
    below = jnp.where(cols < rows, weights, 0.0)
    return below + jnp.where(cols == rows, 1.0, 0.0).astype(F32)


def row_mask(at, z, pattern, rows):
    return pattern[at[0] // 2, (z * NXC + at[2] * NC + at[3]) * rows // BLK].astype(F32)


def root_columns(at, *refs):
    blocks, (whole, columns) = refs[:NXC], refs[NXC:]
    rows, cols = blocks[0].shape
    for k, block in enumerate(blocks):
        core = at[3] if k < NX else 1 - at[3]
        place = lax.rem(at[2] + NX - k % NX, NX) * NC + core
        low = lower_piece(block[...], (at[1] * NXC + place) * rows, at[0] * cols)
        whole[pl.ds(pl.multiple_of(place * rows, rows), rows)] = low
    parts = []
    for b in range(0, cols, NXC * rows):
        pair = whole[:, pl.ds(pl.multiple_of(b + at[2] * NC * rows, NC * rows), NC * rows)]
        parts.append(jnp.where(at[3] == 0, pair[:, :rows], pair[:, rows:]))
    columns[...] = jnp.concatenate(parts, axis=1)


def whole_lower(columns):
    return jnp.concatenate([block[...] for block in columns], axis=1)


def place_chip_blocks(at, blocks, out):
    rows = blocks[0].shape[0]
    for k, block in enumerate(blocks):
        s, core = k % NX, at[3] if k < NX else 1 - at[3]
        chip = lax.rem(at[2] + NX - s, NX)
        out[pl.ds(pl.multiple_of((chip * NC + core) * rows, rows), rows)] = block[...]


def take_nodes(at, stacks, nodes, sem):
    move = pltpu.make_async_copy(stacks.at[:, stacks.shape[1] - nodes.shape[1]:], nodes, sem.at[0])
    move.start()
    move.wait()


def mix(at, pattern, *refs):
    columns, stacks, (keep, give, full, part) = refs[:NY], refs[NY], refs[NY + 2:]
    rows, per_y = keep.shape[1], NZ // NY
    for s in range(NY):
        k = lax.rem(at[0] + NY - s, NY) * per_y
        for b in range(per_y):
            full[(s * per_y + b) * rows:(s * per_y + b + 1) * rows] = stacks[k + b, :rows] * row_mask(at, k + b, pattern, rows)
    part[...] = product(whole_lower(columns), full[...], ROWS)
    for s in range(NX):
        chip = lax.rem(at[2] + NX - s, NX)
        for core, out in ((at[3], keep), (1 - at[3], give)):
            out[s] = part[pl.ds(pl.multiple_of((chip * NC + core) * rows, rows), rows)]


def add_cores(at, keep, got, *outs):
    for s, out in enumerate(outs):
        out[...] = keep[s] + got[s]


def whole_node(at, *refs):
    blocks, out = refs[:NXC], refs[NXC]
    for k, block in enumerate(blocks):
        s, core = k % NX, at[3] if k < NX else 1 - at[3]
        chip = lax.rem(at[2] + NX - s, NX)
        count, width = block.shape[1:]
        for b in range(NZ):
            place = chip * NC + core
            out[b, place] = lower_piece(block[b], (b * NXC + place) * count, at[0] % 2 * width)


def solve(at, own, other, node, out):
    half = at[0] % 2
    width = own.shape[1]
    first = node[pl.ds(pl.multiple_of(half * width, width), width)]
    second = node[pl.ds(pl.multiple_of((1 - half) * width, width), width)]
    out[...] = product(own[...], first, ROWS) + product(other[...], second, ROWS)


def store_by_y(at, value, out, rows):
    per_y = NZ // NY
    for s in range(NY):
        k = lax.rem(at[0] + NY - s, NY) * per_y
        for b in range(per_y):
            at_row = (s * per_y + b) * rows
            out[k + b, :rows] = value[at_row:at_row + rows]


def root_part(at, first, columns, whole, out, part, sem):
    rows, per_y = out.shape[1], NZ // NY
    part[...] = product(whole_lower(columns), whole[...], COLS)
    moves = []
    for s in range(len(columns)):
        k = lax.rem(at[0] + NY - s - first, NY) * per_y
        for b in range(per_y):
            from_rows = part.at[pl.ds((s * per_y + b) * rows, rows)]
            moves.append(pltpu.make_async_copy(from_rows, out.at[k + b], sem.at[len(moves)]))
            moves[-1].start()
    for move in moves:
        move.wait()


def root_product(at, *refs):
    root_part(at, 0, refs[:NY // 2], *refs[NY // 2:])


def root_rest(at, *refs):
    columns, whole, _, out, part, sem = refs[:NY // 2], *refs[NY // 2:]
    root_part(at, NY // 2, columns, whole, out, part, sem)


def choose(at, *refs):
    blocks, (out, full) = refs[:NXC], refs[NXC:]
    place_chip_blocks(at, blocks, full)
    size, take = out.shape[0], out.shape[1] // 2
    node_rows = take * 2 // NZ
    src = lax.broadcasted_iota(jnp.int32, (full.shape[1], take), 0)
    dst = lax.broadcasted_iota(jnp.int32, (full.shape[1], take), 1)
    pick = src == dst // node_rows * (NXC * node_rows) + (at[2] * NC + at[3]) * node_rows + dst % node_rows
    taken = product(full[...], jnp.where(pick, 1.0, 0.0).astype(F32), ROWS)
    out[...] = jnp.concatenate([taken[:size], taken[size:]], axis=1)


def cross_product(at, *refs):
    columns, blocks, (out, full) = refs[:NY], refs[NY:NY + NXC], refs[NY + NXC:]
    place_chip_blocks(at, blocks, full)
    store_by_y(at, product(whole_lower(columns), full[...], COLS), out, blocks[0].shape[0])


def gram_product(at, own, other, *refs):
    blocks, (_, out, full) = refs[:NXC], refs[NXC:]
    place_chip_blocks(at, blocks, full)
    first, take = (at[0] % 2) == 0, own.shape[1] // 2
    mine, his = own[...], other[...]
    low, high = jnp.where(first, mine, his), jnp.where(first, his, mine)
    chosen = jnp.concatenate(
        [
            jnp.concatenate([low[:, :take], high[:, :take]], axis=1),
            jnp.concatenate([low[:, take:], high[:, take:]], axis=1),
        ],
        axis=0,
    )
    out[...] = product(chosen, full[...], COLS).reshape(out.shape)


def finish(at, pattern, got, gram, cross, node):
    total = got[0]
    for k in range(1, NZ):
        total = total + got[k]
    rows = cross.shape[0]
    cross[...] = -(total[:rows] * row_mask(at, at[1], pattern, rows))
    node[...] = gram[...] + total[rows:]


def on_device(root_inverse, level_inverse, coupling, pattern):
    y, z, x, c = (lax.axis_index(name) for name in ("y", "z", "x", "c"))
    grid_index = z * NXC + x * NC + c
    half = y % 2
    rows, cols = root_inverse.shape
    node_rows, width = level_inverse.shape
    at = jnp.stack([y, z, x, c]).astype(jnp.int32)
    per = rows + node_rows
    smem, vmem, anywhere = (pl.BlockSpec(memory_space=m) for m in (pltpu.SMEM, pltpu.VMEM, pl.ANY))
    outside = pl.BlockSpec(memory_space=pltpu.HBM)

    blocks = chip_blocks(root_inverse)
    stacks = jnp.broadcast_to(jnp.concatenate([coupling, level_inverse])[None], (NZ, per, width))
    stacks = lax.all_to_all(stacks, "z", 0, 0, tiled=True)
    nodes = call(take_nodes, [(NZ, node_rows, width)], in_specs=[smem, anywhere], copies=1)(at, stacks)[0]
    nodes = chip_blocks(nodes)
    whole, columns = call(root_columns, [(NXC * rows, cols), (NXC * rows, cols // NXC)], n_in=NXC)(
        at, *blocks
    )
    columns = [columns] + [shifted(columns, "y", s) for s in range(1, NY)]

    shape, part = [(NZ, rows, cols)], [(NZ // 2 * rows, cols)]
    root = call(
        root_product, shape, part, NY // 2 + 1, out_specs=[outside], copies=NZ // 2
    )(at, *columns[:NY // 2], whole)[0]
    root = call(
        root_rest,
        shape,
        part,
        in_specs=[smem] + [vmem] * (NY // 2 + 1) + [outside],
        out_specs=[outside],
        aliases={NY // 2 + 2: 0},
        copies=NZ // 2,
        weight=17_000_000_000,
    )(at, *columns[NY // 2:], whole, root)[0]
    summed = lax.all_to_all(root, "z", 0, 0, tiled=True)

    keep, give = call(
        mix,
        [(NX, rows, width)] * 2,
        [(NZ * rows, width), (NXC * rows, width)],
        in_specs=[smem, smem] + [vmem] * (NY + 1) + [anywhere],
    )(at, pattern, *columns, stacks, root)
    parts = call(add_cores, [(rows, width)] * NX, n_in=2)(at, keep, from_partner(give, "c"))
    mixed = parts[0]
    for s in range(1, NX):
        mixed = mixed + shifted(parts[s], "x", -s)

    node_all = call(whole_node, [(NZ, NXC, node_rows, width)], n_in=NXC)(at, *nodes)[0]
    node_all = node_all.reshape(NZ * NXC * node_rows, width)
    solved = call(solve, [(rows, width)], n_in=3, weight=25_000_000_000)(at, mixed, from_partner(mixed, "y"), node_all)[0]
    solved = chip_blocks(solved)

    own = call(choose, [(NX * rows, 2 * width // NXC)], [(NXC * rows, width)], NXC)(at, *solved)[0]
    both = call(cross_product, [(NZ, per, width)], [(NXC * rows, width)], NY + NXC)(at, *columns, *solved)[0]
    both = call(
        gram_product,
        [(NZ, per, width)],
        [(NXC * rows, width)],
        aliases={3 + NXC: 0},
        in_specs=[smem] + [vmem] * (2 + NXC) + [anywhere],
        out_specs=[pl.BlockSpec((NZ, node_rows, width), lambda i: (0, rows // node_rows, 0))],
        grid=(1,),
    )(at, own, from_partner(own, "y"), *solved, both)[0]
    both, summed = lax.optimization_barrier((both, summed))
    both = lax.all_to_all(both, "z", 0, 0, tiled=True)

    per_half = width // node_rows
    mine = lax.dynamic_slice_in_dim(node_all, grid_index % per_half * node_rows, node_rows, 1).T
    mine = jnp.where(grid_index // per_half == half, mine, from_partner(mine, "y"))
    node_gram = jnp.dot(mine, node_all, precision=lax.Precision.HIGHEST, preferred_element_type=F32)
    cross_cov, node_cov = call(finish, [(rows, width), (node_rows, width)], in_specs=[smem, smem, vmem, vmem])(
        at, pattern, both, node_gram
    )
    return jnp.sum(summed, axis=0), cross_cov, node_cov


def solution(mesh):
    split = Mesh(mesh.devices.reshape(NY, NZ, NX, NC), ("y", "z", "x", "c"))
    placed = P(("z", "x", "c"), "y")
    return jax.shard_map(
        on_device,
        mesh=split,
        in_specs=(placed, placed, placed, P()),
        out_specs=(placed, placed, placed),
        check_vma=False,
    )
```

```python
import jax
import jax.numpy as jnp
from jax import lax
from jax.experimental import pallas as pl
from jax.experimental.pallas import tpu as pltpu
from jax.sharding import Mesh, PartitionSpec as P

BLK = 128
NY, NZ, NX, NC = 4, 8, 4, 2
NXC = NX * NC
F32 = jnp.float32


def shifted(value, axis, step):
    size = lax.axis_size(axis)
    return lax.ppermute(value, axis, [(i, (i + step) % size) for i in range(size)])


def from_partner(value, axis):
    return lax.ppermute(value, axis, [(i, i ^ 1) for i in range(lax.axis_size(axis))])


def chip_blocks(value):
    own = [value] + [shifted(value, "x", s) for s in range(1, NX)]
    return own + [from_partner(block, "c") for block in own]


def halves(value):
    high = value.astype(jnp.bfloat16)
    return high, (value - high.astype(F32)).astype(jnp.bfloat16)


def product(left, right, contracting):
    (high, low), (right_high, right_low) = halves(left), halves(right)

    def dot(p, q):
        return lax.dot_general(p, q, (contracting, ((), ())), preferred_element_type=F32)

    return dot(high, right_high) + (dot(high, right_low) + dot(low, right_high))


ROWS = ((1,), (0,))
COLS = ((0,), (0,))


def call(body, outs, scratch=(), n_in=1, aliases=None, in_specs=None, out_specs=None, grid=(), copies=0, weight=0):
    vmem = pl.BlockSpec(memory_space=pltpu.VMEM)
    smem = pl.BlockSpec(memory_space=pltpu.SMEM)
    return pl.pallas_call(
        body,
        out_shape=[jax.ShapeDtypeStruct(shape, F32) for shape in outs],
        in_specs=in_specs or [smem] + [vmem] * n_in,
        out_specs=out_specs or [vmem] * len(outs),
        grid=grid,
        scratch_shapes=[pltpu.VMEM(shape, F32) for shape in scratch]
        + ([pltpu.SemaphoreType.DMA((copies,))] if copies else []),
        input_output_aliases=aliases or {},
        cost_estimate=pl.CostEstimate(flops=weight, transcendentals=0, bytes_accessed=0) if weight else None,
        compiler_params=pltpu.CompilerParams(vmem_limit_bytes=48 * 2**20),
    )


def lower_piece(weights, row_start, col_start):
    rows = row_start + lax.broadcasted_iota(jnp.int32, weights.shape, 0)
    cols = col_start + lax.broadcasted_iota(jnp.int32, weights.shape, 1)
    below = jnp.where(cols < rows, weights, 0.0)
    return below + jnp.where(cols == rows, 1.0, 0.0).astype(F32)


def row_mask(at, z, pattern, rows):
    return pattern[at[0] // 2, (z * NXC + at[2] * NC + at[3]) * rows // BLK].astype(F32)


def root_columns(at, *refs):
    blocks, (whole, columns) = refs[:NXC], refs[NXC:]
    rows, cols = blocks[0].shape
    for k, block in enumerate(blocks):
        core = at[3] if k < NX else 1 - at[3]
        place = lax.rem(at[2] + NX - k % NX, NX) * NC + core
        low = lower_piece(block[...], (at[1] * NXC + place) * rows, at[0] * cols)
        whole[pl.ds(pl.multiple_of(place * rows, rows), rows)] = low
    parts = []
    for b in range(0, cols, NXC * rows):
        pair = whole[:, pl.ds(pl.multiple_of(b + at[2] * NC * rows, NC * rows), NC * rows)]
        parts.append(jnp.where(at[3] == 0, pair[:, :rows], pair[:, rows:]))
    columns[...] = jnp.concatenate(parts, axis=1)


def whole_lower(columns):
    return jnp.concatenate([block[...] for block in columns], axis=1)


def place_chip_blocks(at, blocks, out):
    rows = blocks[0].shape[0]
    for k, block in enumerate(blocks):
        s, core = k % NX, at[3] if k < NX else 1 - at[3]
        chip = lax.rem(at[2] + NX - s, NX)
        out[pl.ds(pl.multiple_of((chip * NC + core) * rows, rows), rows)] = block[...]


def take_nodes(at, stacks, nodes, sem):
    move = pltpu.make_async_copy(stacks.at[:, stacks.shape[1] - nodes.shape[1]:], nodes, sem.at[0])
    move.start()
    move.wait()


def mix(at, pattern, *refs):
    columns, stacks, (keep, give, full, part) = refs[:NY], refs[NY], refs[NY + 2:]
    rows, per_y = keep.shape[1], NZ // NY
    for s in range(NY):
        k = lax.rem(at[0] + NY - s, NY) * per_y
        for b in range(per_y):
            full[(s * per_y + b) * rows:(s * per_y + b + 1) * rows] = stacks[k + b, :rows] * row_mask(at, k + b, pattern, rows)
    part[...] = product(whole_lower(columns), full[...], ROWS)
    for s in range(NX):
        chip = lax.rem(at[2] + NX - s, NX)
        for core, out in ((at[3], keep), (1 - at[3], give)):
            out[s] = part[pl.ds(pl.multiple_of((chip * NC + core) * rows, rows), rows)]


def add_cores(at, keep, got, *outs):
    for s, out in enumerate(outs):
        out[...] = keep[s] + got[s]


def whole_node(at, *refs):
    blocks, out = refs[:NXC], refs[NXC]
    for k, block in enumerate(blocks):
        s, core = k % NX, at[3] if k < NX else 1 - at[3]
        chip = lax.rem(at[2] + NX - s, NX)
        count, width = block.shape[1:]
        for b in range(NZ):
            place = chip * NC + core
            out[b, place] = lower_piece(block[b], (b * NXC + place) * count, at[0] % 2 * width)


def solve(at, own, other, node, out):
    half = at[0] % 2
    width = own.shape[1]
    first = node[pl.ds(pl.multiple_of(half * width, width), width)]
    second = node[pl.ds(pl.multiple_of((1 - half) * width, width), width)]
    out[...] = product(own[...], first, ROWS) + product(other[...], second, ROWS)


def store_by_y(at, value, out, rows):
    per_y = NZ // NY
    for s in range(NY):
        k = lax.rem(at[0] + NY - s, NY) * per_y
        for b in range(per_y):
            at_row = (s * per_y + b) * rows
            out[k + b, :rows] = value[at_row:at_row + rows]


def root_part(at, first, columns, whole, out, part, sem):
    rows, per_y = out.shape[1], NZ // NY
    part[...] = product(whole_lower(columns), whole[...], COLS)
    moves = []
    for s in range(len(columns)):
        k = lax.rem(at[0] + NY - s - first, NY) * per_y
        for b in range(per_y):
            from_rows = part.at[pl.ds((s * per_y + b) * rows, rows)]
            moves.append(pltpu.make_async_copy(from_rows, out.at[k + b], sem.at[len(moves)]))
            moves[-1].start()
    for move in moves:
        move.wait()


def root_product(at, *refs):
    root_part(at, 0, refs[:NY // 2], *refs[NY // 2:])


def root_rest(at, *refs):
    columns, whole, _, out, part, sem = refs[:NY // 2], *refs[NY // 2:]
    root_part(at, NY // 2, columns, whole, out, part, sem)


def choose(at, *refs):
    blocks, (out, full) = refs[:NXC], refs[NXC:]
    place_chip_blocks(at, blocks, full)
    size, take = out.shape[0], out.shape[1] // 2
    node_rows = take * 2 // NZ
    src = lax.broadcasted_iota(jnp.int32, (full.shape[1], take), 0)
    dst = lax.broadcasted_iota(jnp.int32, (full.shape[1], take), 1)
    pick = src == dst // node_rows * (NXC * node_rows) + (at[2] * NC + at[3]) * node_rows + dst % node_rows
    pick = jnp.where(pick, 1.0, 0.0).astype(jnp.bfloat16)
    high, low = (lax.dot_general(part, pick, (ROWS, ((), ())), preferred_element_type=F32) for part in halves(full[...]))
    taken = high + low
    out[...] = jnp.concatenate([taken[:size], taken[size:]], axis=1)


def cross_product(at, *refs):
    columns, blocks, (out, full) = refs[:NY], refs[NY:NY + NXC], refs[NY + NXC:]
    place_chip_blocks(at, blocks, full)
    store_by_y(at, product(whole_lower(columns), full[...], COLS), out, blocks[0].shape[0])


def gram_product(at, own, other, *refs):
    blocks, (_, out, full) = refs[:NXC], refs[NXC:]
    place_chip_blocks(at, blocks, full)
    first, take = (at[0] % 2) == 0, own.shape[1] // 2
    mine, his = own[...], other[...]
    low, high = jnp.where(first, mine, his), jnp.where(first, his, mine)
    chosen = jnp.concatenate(
        [
            jnp.concatenate([low[:, :take], high[:, :take]], axis=1),
            jnp.concatenate([low[:, take:], high[:, take:]], axis=1),
        ],
        axis=0,
    )
    out[...] = product(chosen, full[...], COLS).reshape(out.shape)


def finish(at, pattern, got, gram, cross, node):
    total = got[0]
    for k in range(1, NZ):
        total = total + got[k]
    rows = cross.shape[0]
    cross[...] = -(total[:rows] * row_mask(at, at[1], pattern, rows))
    node[...] = gram[...] + total[rows:]


def on_device(root_inverse, level_inverse, coupling, pattern):
    y, z, x, c = (lax.axis_index(name) for name in ("y", "z", "x", "c"))
    grid_index = z * NXC + x * NC + c
    half = y % 2
    rows, cols = root_inverse.shape
    node_rows, width = level_inverse.shape
    at = jnp.stack([y, z, x, c]).astype(jnp.int32)
    per = rows + node_rows
    smem, vmem, anywhere = (pl.BlockSpec(memory_space=m) for m in (pltpu.SMEM, pltpu.VMEM, pl.ANY))
    outside = pl.BlockSpec(memory_space=pltpu.HBM)

    blocks = chip_blocks(root_inverse)
    stacks = jnp.broadcast_to(jnp.concatenate([coupling, level_inverse])[None], (NZ, per, width))
    stacks = lax.all_to_all(stacks, "z", 0, 0, tiled=True)
    nodes = call(take_nodes, [(NZ, node_rows, width)], in_specs=[smem, anywhere], copies=1)(at, stacks)[0]
    nodes = chip_blocks(nodes)
    whole, columns = call(root_columns, [(NXC * rows, cols), (NXC * rows, cols // NXC)], n_in=NXC)(
        at, *blocks
    )
    columns = [columns] + [shifted(columns, "y", s) for s in range(1, NY)]

    shape, part = [(NZ, rows, cols)], [(NZ // 2 * rows, cols)]
    root = call(
        root_product, shape, part, NY // 2 + 1, out_specs=[outside], copies=NZ // 2
    )(at, *columns[:NY // 2], whole)[0]
    root = call(
        root_rest,
        shape,
        part,
        in_specs=[smem] + [vmem] * (NY // 2 + 1) + [outside],
        out_specs=[outside],
        aliases={NY // 2 + 2: 0},
        copies=NZ // 2,
        weight=17_000_000_000,
    )(at, *columns[NY // 2:], whole, root)[0]
    summed = lax.all_to_all(root, "z", 0, 0, tiled=True)

    keep, give = call(
        mix,
        [(NX, rows, width)] * 2,
        [(NZ * rows, width), (NXC * rows, width)],
        in_specs=[smem, smem] + [vmem] * (NY + 1) + [anywhere],
    )(at, pattern, *columns, stacks, root)
    parts = call(add_cores, [(rows, width)] * NX, n_in=2)(at, keep, from_partner(give, "c"))
    mixed = parts[0]
    for s in range(1, NX):
        mixed = mixed + shifted(parts[s], "x", -s)

    node_all = call(whole_node, [(NZ, NXC, node_rows, width)], n_in=NXC)(at, *nodes)[0]
    node_all = node_all.reshape(NZ * NXC * node_rows, width)
    solved = call(solve, [(rows, width)], n_in=3, weight=25_000_000_000)(at, mixed, from_partner(mixed, "y"), node_all)[0]
    solved = chip_blocks(solved)

    own = call(choose, [(NX * rows, 2 * width // NXC)], [(NXC * rows, width)], NXC)(at, *solved)[0]
    both = call(cross_product, [(NZ, per, width)], [(NXC * rows, width)], NY + NXC)(at, *columns, *solved)[0]
    both = call(
        gram_product,
        [(NZ, per, width)],
        [(NXC * rows, width)],
        aliases={3 + NXC: 0},
        in_specs=[smem] + [vmem] * (2 + NXC) + [anywhere],
        out_specs=[pl.BlockSpec((NZ, node_rows, width), lambda i: (0, rows // node_rows, 0))],
        grid=(1,),
    )(at, own, from_partner(own, "y"), *solved, both)[0]
    both, summed = lax.optimization_barrier((both, summed))
    both = lax.all_to_all(both, "z", 0, 0, tiled=True)

    per_half = width // node_rows
    mine = lax.dynamic_slice_in_dim(node_all, grid_index % per_half * node_rows, node_rows, 1).T
    mine = jnp.where(grid_index // per_half == half, mine, from_partner(mine, "y"))
    node_gram = jnp.dot(mine, node_all, precision=lax.Precision.HIGHEST, preferred_element_type=F32)
    cross_cov, node_cov = call(finish, [(rows, width), (node_rows, width)], in_specs=[smem, smem, vmem, vmem])(
        at, pattern, both, node_gram
    )
    return jnp.sum(summed, axis=0), cross_cov, node_cov


def solution(mesh):
    split = Mesh(mesh.devices.reshape(NY, NZ, NX, NC), ("y", "z", "x", "c"))
    placed = P(("z", "x", "c"), "y")
    return jax.shard_map(
        on_device,
        mesh=split,
        in_specs=(placed, placed, placed, P()),
        out_specs=(placed, placed, placed),
        check_vma=False,
    )
```
